32 devices in a mesh: groups: 2 (over x), loop: 16 (over z, y, core).
Axes of the slice: x: 2, y: 2, z: 4, core: 2. Of those that a mesh axis runs over, the one named last changes fastest.
Arguments:
- embeddings: bfloat16 [4096, 1024], P(('groups', 'loop')), parts along dimension 0
- generation: int32 [4096], P(('groups', 'loop')), parts along dimension 0, may hold values from 0 to 2047, as said below
- eligible: int32 [4096], P(('groups', 'loop')), parts along dimension 0, may hold values 0 or 1
Outputs:
- neighbour: bfloat16 [4096, 1024], P(('groups', 'loop')), parts along dimension 0
- row_max: float32 [4096], P(('groups', 'loop')), parts along dimension 0
The draws below stay inside these ranges and needn't reach their ends.
There are 2 independent parts, one for each index of `groups`. The reference program is written for one: setup_inputs(seed, part) draws one part's arguments, and reference() takes and returns one part's arrays. A program takes and returns all parts, laid end to end along the dimension named above; each array names one. Nothing has to cross between parts.
Inputs may be any that keep to these rules, and one draw needn't show every extreme that they name: generation is a permutation of 0 to 2047; loop index d holds the generation indices d * 64 to d * 64 + 63 in its first 64 rows and (31 - d) * 64 to (32 - d) * 64 - 1 in its last 64 rows, in any order within each block.
All inputs are finite; a program needn't handle non-finite values. No bound on the sum of `eligible` on one device may be relied on, other than what follows from the above.
Results may differ from the reference program's by a relative error of at most 0.0035.
Values may be sent and summed in bfloat16 or wider, within the bound.
No kernel may reach another device: no remote copies, remote signals or barrier semaphores. Data moves between devices by JAX's collectives and lax.ppermute only.
A program may use at most 128 MiB of HBM per device.

```python
import math
import jax
import jax.numpy as jnp
from jax import lax

VECTOR_LENGTH = 1024
ROWS_DEV = 128
ROWS = 2048
N_LOOP = 16


def draw_embeddings(key, part):
    rows = ROWS_DEV * N_LOOP
    key_base = jax.random.fold_in(key, 0)
    values = jnp.clip(jax.random.normal(key_base, (rows, VECTOR_LENGTH), jnp.float32), -6.0, 6.0)
    return values.astype(jnp.bfloat16)


def draw_generation(key, part):
    half_rows = ROWS_DEV // 2
    blocks = 2 * N_LOOP
    orders = jax.vmap(lambda single: jax.random.permutation(single, half_rows))(jax.random.split(key, blocks))
    device = jnp.arange(N_LOOP)
    block_ids = jnp.stack([device, 2 * N_LOOP - 1 - device], axis=1).reshape(-1)
    values = block_ids[:, None] * half_rows + orders
    return values.reshape(-1).astype(jnp.int32)


def with_ends(entries, rng, least, top_value):
    dims = entries.shape
    index_at = [jax.random.randint(jax.random.fold_in(rng, axis), (), 0, dims[axis]) for axis in range(len(dims))]
    entries = entries.at[tuple(index_at)].set(least)
    longest = dims.index(max(dims))
    index_at[longest] = (index_at[longest] + 1) % dims[longest]
    return entries.at[tuple(index_at)].set(top_value)


def setup_inputs(seed: int = 0, part: int = 0) -> dict:
    keys = jax.random.split(jax.random.key(seed), 4)
    part_keys = jax.random.split(jax.random.fold_in(keys[3], part), 4)
    embeddings = draw_embeddings(jax.random.fold_in(jax.random.fold_in(keys[3], part), 71), part)
    generation = draw_generation(jax.random.fold_in(jax.random.fold_in(keys[3], part), 71), part)
    eligible = with_ends((jax.random.randint(part_keys[2], (ROWS,), 0, 4) < 3).astype(jnp.int32), jax.random.fold_in(part_keys[2], 1), 0, 1)
    return dict(embeddings=embeddings, generation=generation, eligible=eligible)


smoothing_divisor = 3.0

def reference(embeddings, generation, eligible):
    normalizer_multiplier = smoothing_divisor / math.sqrt(VECTOR_LENGTH)
    total_rows = embeddings.shape[0]
    step_rows = math.gcd(total_rows, 512)
    usable = eligible == 1

    def block(start):
        queries = lax.dynamic_slice_in_dim(embeddings, start, step_rows, 0)
        query_gen = lax.dynamic_slice_in_dim(generation, start, step_rows, 0)
        scores = jnp.dot(queries, embeddings.T, preferred_element_type=jnp.float32) * normalizer_multiplier
        valid = (generation[None, :] < query_gen[:, None]) & usable[None, :]
        masked = jnp.where(valid, scores, -jnp.inf)
        peak = jnp.maximum(lax.optimization_barrier(jnp.max(masked, axis=1)), jnp.float32(0.0))
        expo = jnp.where(valid, jnp.exp(scores - peak[:, None]), jnp.float32(0.0))
        total = jnp.exp(-peak) + lax.optimization_barrier(jnp.sum(expo, axis=1))
        running_sum = jnp.dot(expo.astype(jnp.bfloat16), embeddings, preferred_element_type=jnp.float32)
        return ((running_sum / total[:, None]).astype(jnp.bfloat16), peak)
    starts = (jnp.arange(total_rows // step_rows) * step_rows).astype(jnp.int32)
    output_rows, peaks = lax.map(block, starts)
    return (output_rows.reshape(total_rows, embeddings.shape[1]), peaks.reshape(total_rows))
```

```python
import functools
import math

import jax
import jax.numpy as jnp
import numpy as np
from jax import lax
from jax.experimental import pallas as pl
from jax.experimental.pallas import tpu as pltpu
from jax.sharding import PartitionSpec as P

smoothing_divisor = 3.0


def ring_of_chips(chips):
    across = max(k for k in range(1, int(math.isqrt(chips)) + 1) if chips % k == 0)
    down = chips // across
    order = [(0, 0)]
    for r in range(down):
        columns = range(1, across)
        order += [(r, q) for q in (columns if r % 2 == 0 else reversed(columns))]
    order += [(r, 0) for r in range(down - 1, 0, -1)]
    return [r * across + q for r, q in order]


def swaps(ring):
    size = len(ring)
    even, odd = {}, {}
    for k in range(size):
        even[ring[k]] = ring[k ^ 1]
        odd[ring[k]] = ring[(((k - 1) ^ 1) + 1) % size]
    return even, odd


def attend_kernel(mult, me_ref, table_ref, x_ref, gen_ref, flag_ref, *refs):
    rows = x_ref.shape[0]
    half = rows // 2
    chunks, (out_ref, peak_ref, score_ref) = refs[:-3], refs[-3:]
    me = me_ref[0]
    x = x_ref[...]
    row_id = lax.broadcasted_iota(jnp.int32, (rows, rows), 0)
    col_id = lax.broadcasted_iota(jnp.int32, (rows, rows), 1)
    eye = row_id == col_id
    late_q, late_k = row_id >= half, col_id >= half
    gen_k = jnp.broadcast_to(gen_ref[...], (rows, rows))
    gen_q = jnp.sum(jnp.where(eye, gen_k, 0), axis=1, keepdims=True)
    dims = (((1,), (1,)), ((), ()))
    peak = jnp.zeros((rows, 1), jnp.float32)
    for k in range(len(chunks) + 1):
        keys = x if k == 0 else chunks[k - 1][...]
        s = lax.dot_general(x, keys, dims, preferred_element_type=jnp.float32) * mult
        if k == 0:
            valid = (gen_k < gen_q) & (jnp.broadcast_to(flag_ref[...], (rows, rows)) == 1)
        else:
            shift = jnp.full((rows, rows), table_ref[me, k] - me)
            early = (~late_k) & (late_q | (shift < 0))
            valid = (early | (late_q & late_k & (shift > 0))) & (s == s)
        s = jnp.where(valid, s, -jnp.inf)
        score_ref[:, k * rows:(k + 1) * rows] = s
        peak = jnp.maximum(peak, jnp.max(s, axis=1, keepdims=True))
    total = jnp.exp(-peak)
    acc = [None, None]
    edge = 2 * rows
    for k in range(0, len(chunks) + 1, 2):
        expo = jnp.exp(score_ref[:, k * rows:(k + 2) * rows] - peak)
        total = total + jnp.sum(expo, axis=1, keepdims=True)
        w = expo.astype(jnp.bfloat16)
        pair = [x_ref if j == 0 else chunks[j - 1] for j in (k, k + 1)]
        head = jnp.concatenate([r[:, :edge] for r in pair], axis=0)
        head = jnp.where(head == head, head, jnp.zeros_like(head))
        tail = jnp.concatenate([r[:, edge:] for r in pair], axis=0)
        for i, v in enumerate((head, tail)):
            t = jnp.dot(w, v, preferred_element_type=jnp.float32)
            acc[i] = t if acc[i] is None else acc[i] + t
    out_ref[:, :edge] = (acc[0] / total).astype(out_ref.dtype)
    out_ref[:, edge:] = (acc[1] / total).astype(out_ref.dtype)
    peak_ref[...] = jnp.sum(jnp.where(eye, peak, 0.0), axis=0, keepdims=True)


def ring_body(n, embeddings, generation, eligible):
    rows, width = embeddings.shape
    mult = smoothing_divisor / math.sqrt(width)
    ring = ring_of_chips(n // 2)
    maps = swaps(ring)
    me = lax.axis_index("loop")

    def swap(kind, v):
        return lax.ppermute(v, "loop", [(i, maps[kind][i // 2] * 2 + i % 2) for i in range(n)])

    def other_core(v):
        return lax.ppermute(v, "loop", [(i, i ^ 1) for i in range(n)])

    first = lax.broadcasted_iota(jnp.int32, (rows, width), 1) == 0
    coded = jnp.where(first & (eligible[:, None] != 1), jnp.bfloat16(jnp.nan), embeddings)

    got = [(coded, [])]
    held = [coded, coded]
    steps = n // 4
    for step in range(steps):
        sent = [held[1], held[0]] if step else held
        if step == steps - 1:
            sent = [sent[0][: rows // 2], sent[1][rows // 2 :]]
        held = [swap(kind, sent[kind]) for kind in (0, 1)]
        paths = [[(kind + k) % 2 for k in range(step + 1)] for kind in (0, 1)]
        if step == steps - 1:
            got.append((jnp.concatenate(held, axis=0), paths[0]))
        else:
            got += list(zip(held, paths))
    chunks, table = [], np.zeros((n, n), np.int32)
    for k, (v, path) in enumerate(got):
        chunks += [v, other_core(v)] if k else [other_core(v)]
        for i in range(n):
            chip = i // 2
            for kind in path:
                chip = maps[kind][chip]
            table[i, 2 * k : 2 * k + 2] = chip * 2 + i % 2, chip * 2 + 1 - i % 2
    vmem = pl.BlockSpec(memory_space=pltpu.VMEM)
    out, peak = pl.pallas_call(
        functools.partial(attend_kernel, mult),
        out_shape=(
            jax.ShapeDtypeStruct((rows, width), jnp.bfloat16),
            jax.ShapeDtypeStruct((1, rows), jnp.float32),
        ),
        in_specs=[pl.BlockSpec(memory_space=pltpu.SMEM)] * 2 + [vmem] * (3 + len(chunks)),
        out_specs=(vmem, vmem),
        scratch_shapes=[pltpu.VMEM((rows, n * rows), jnp.float32)],
        name="attend",
    )(me.reshape(1), jnp.asarray(table), embeddings, generation.reshape(1, rows), eligible.reshape(1, rows), *chunks)
    return out, peak.reshape(rows)


def gathered_body(embeddings, generation, eligible):
    rows, width = embeddings.shape
    mult = smoothing_divisor / math.sqrt(width)
    keys = lax.all_gather(embeddings, "loop", axis=0, tiled=True)
    key_gen = lax.all_gather(generation, "loop", axis=0, tiled=True)
    key_flag = lax.all_gather(eligible, "loop", axis=0, tiled=True)
    scores = jnp.dot(embeddings, keys.T, preferred_element_type=jnp.float32) * mult
    valid = (key_gen[None, :] < generation[:, None]) & (key_flag[None, :] == 1)
    masked = jnp.where(valid, scores, -jnp.inf)
    peak = jnp.maximum(jnp.max(masked, axis=1), 0.0)
    expo = jnp.where(valid, jnp.exp(scores - peak[:, None]), jnp.float32(0.0))
    total = jnp.exp(-peak) + jnp.sum(expo, axis=1)
    summed = jnp.dot(expo.astype(jnp.bfloat16), keys, preferred_element_type=jnp.float32)
    return (summed / total[:, None]).astype(jnp.bfloat16), peak


def solution(mesh):
    n = mesh.shape["loop"]
    body = functools.partial(ring_body, n) if n <= 16 else gathered_body
    placed = (P(("groups", "loop"), None), P(("groups", "loop")), P(("groups", "loop")))
    return jax.shard_map(
        body,
        mesh=mesh,
        in_specs=placed,
        out_specs=(P(("groups", "loop"), None), P(("groups", "loop"))),
        check_vma=False,
    )
```

```python
import functools
import math

import jax
import jax.numpy as jnp
import numpy as np
from jax import lax
from jax.experimental import pallas as pl
from jax.experimental.pallas import tpu as pltpu
from jax.sharding import PartitionSpec as P

smoothing_divisor = 3.0


def ring_of_chips(chips):
    across = max(k for k in range(1, int(math.isqrt(chips)) + 1) if chips % k == 0)
    down = chips // across
    order = [(0, 0)]
    for r in range(down):
        columns = range(1, across)
        order += [(r, q) for q in (columns if r % 2 == 0 else reversed(columns))]
    order += [(r, 0) for r in range(down - 1, 0, -1)]
    return [r * across + q for r, q in order]


def swaps(ring):
    size = len(ring)
    even, odd = {}, {}
    for k in range(size):
        even[ring[k]] = ring[k ^ 1]
        odd[ring[k]] = ring[(((k - 1) ^ 1) + 1) % size]
    return even, odd


def code_kernel(x_ref, flag_ref, *out_refs):
    rows = x_ref.shape[0]
    half = rows // len(out_refs)
    row_id = lax.broadcasted_iota(jnp.int32, (rows, rows), 0)
    col_id = lax.broadcasted_iota(jnp.int32, (rows, rows), 1)
    flags = jnp.broadcast_to(flag_ref[...], (rows, rows))
    flag = jnp.sum(jnp.where(row_id == col_id, flags, 0), axis=1, keepdims=True)
    bad = (flag != 1) & (lax.broadcasted_iota(jnp.int32, (rows, 128), 1) == 0)
    head = jnp.where(bad, jnp.float32(jnp.nan), x_ref[:, :128].astype(jnp.float32)).astype(jnp.bfloat16)
    for k, out_ref in enumerate(out_refs):
        out_ref[:, :128] = head[k * half : (k + 1) * half]
        out_ref[:, 128:] = x_ref[k * half : (k + 1) * half, 128:]


def attend_kernel(mult, me_ref, table_ref, x_ref, gen_ref, flag_ref, *refs):
    rows = x_ref.shape[0]
    half = rows // 2
    chunks, (out_ref, peak_ref, score_ref) = refs[:-3], refs[-3:]
    me = me_ref[0]
    x = x_ref[...]
    row_id = lax.broadcasted_iota(jnp.int32, (rows, rows), 0)
    col_id = lax.broadcasted_iota(jnp.int32, (rows, rows), 1)
    eye = row_id == col_id
    late_q, late_k = row_id >= half, col_id >= half
    gen_k = jnp.broadcast_to(gen_ref[...], (rows, rows))
    gen_q = jnp.sum(jnp.where(eye, gen_k, 0), axis=1, keepdims=True)
    dims = (((1,), (1,)), ((), ()))
    peak = jnp.zeros((rows, 1), jnp.float32)
    for k in range(len(chunks) // 2 + 1):
        keys = x if k == 0 else jnp.concatenate([r[...] for r in chunks[2 * k - 2 : 2 * k]], axis=0)
        s = lax.dot_general(x, keys, dims, preferred_element_type=jnp.float32) * mult
        if k == 0:
            valid = (gen_k < gen_q) & (jnp.broadcast_to(flag_ref[...], (rows, rows)) == 1)
        else:
            shift = jnp.full((rows, rows), table_ref[me, k] - me)
            early = (~late_k) & (late_q | (shift < 0))
            valid = (early | (late_q & late_k & (shift > 0))) & (s == s)
        s = jnp.where(valid, s, -jnp.inf)
        score_ref[:, k * rows : (k + 1) * rows] = s
        peak = jnp.maximum(peak, jnp.max(s, axis=1, keepdims=True))
    total = jnp.exp(-peak)
    acc = [None, None]
    edge = 2 * rows
    for k in range(0, len(chunks) // 2 + 1, 2):
        expo = jnp.exp(score_ref[:, k * rows : (k + 2) * rows] - peak)
        total = total + jnp.sum(expo, axis=1, keepdims=True)
        w = expo.astype(jnp.bfloat16)
        group = [x_ref, *chunks[:2]] if k == 0 else chunks[2 * k - 2 : 2 * k + 2]
        head = jnp.concatenate([r[:, :edge] for r in group], axis=0)
        head = jnp.where(head == head, head, jnp.zeros_like(head))
        tail = jnp.concatenate([r[:, edge:] for r in group], axis=0)
        for i, v in enumerate((head, tail)):
            t = jnp.dot(w, v, preferred_element_type=jnp.float32)
            acc[i] = t if acc[i] is None else acc[i] + t
    out_ref[:, :edge] = (acc[0] / total).astype(out_ref.dtype)
    out_ref[:, edge:] = (acc[1] / total).astype(out_ref.dtype)
    peak_ref[...] = jnp.sum(jnp.where(eye, peak, 0.0), axis=0, keepdims=True)


def ring_body(n, embeddings, generation, eligible):
    rows, width = embeddings.shape
    half = rows // 2
    mult = smoothing_divisor / math.sqrt(width)
    maps = swaps(ring_of_chips(n // 2))
    me = lax.axis_index("loop")
    flags = eligible.reshape(1, rows)
    vmem = pl.BlockSpec(memory_space=pltpu.VMEM)
    smem = pl.BlockSpec(memory_space=pltpu.SMEM)
    half_shape = jax.ShapeDtypeStruct((half, width), jnp.bfloat16)

    def swap(kind, v):
        return lax.ppermute(v, "loop", [(i, maps[kind][i // 2] * 2 + i % 2) for i in range(n)])

    def other_core(v):
        return lax.ppermute(v, "loop", [(i, i ^ 1) for i in range(n)])

    coded = pl.pallas_call(
        code_kernel,
        out_shape=(half_shape, half_shape),
        in_specs=[vmem, vmem],
        out_specs=(vmem, vmem),
        compiler_params=pltpu.CompilerParams(vmem_limit_bytes=4 << 20),
        name="code",
    )(embeddings, flags)

    got = [(list(coded), [])]
    held = [list(coded), list(coded)]
    steps = n // 4
    for step in range(steps):
        sent = [held[1], held[0]] if step else held
        paths = [[(kind + k) % 2 for k in range(step + 1)] for kind in (0, 1)]
        if step == steps - 1:
            got.append(([swap(0, sent[0][0]), swap(1, sent[1][1])], paths[0]))
        else:
            held = [[None, None], [None, None]]
            for part in (0, 1):
                for kind in (0, 1):
                    held[kind][part] = swap(kind, sent[kind][part])
            got += list(zip(held, paths))
    chunks, table = [], np.zeros((n, n), np.int32)
    for k, (parts, path) in enumerate(got):
        if k:
            chunks += parts
        chunks += [other_core(v) for v in parts]
        for i in range(n):
            chip = i // 2
            for kind in path:
                chip = maps[kind][chip]
            table[i, 2 * k : 2 * k + 2] = chip * 2 + i % 2, chip * 2 + 1 - i % 2
    out, peak = pl.pallas_call(
        functools.partial(attend_kernel, mult),
        out_shape=(
            jax.ShapeDtypeStruct((rows, width), jnp.bfloat16),
            jax.ShapeDtypeStruct((1, rows), jnp.float32),
        ),
        in_specs=[smem] * 2 + [vmem] * (3 + len(chunks)),
        out_specs=(vmem, vmem),
        scratch_shapes=[pltpu.VMEM((rows, n * rows), jnp.float32)],
        compiler_params=pltpu.CompilerParams(vmem_limit_bytes=24 << 20),
        name="attend",
    )(me.reshape(1), jnp.asarray(table), embeddings, generation.reshape(1, rows), flags, *chunks)
    return out, peak.reshape(rows)


def gathered_body(embeddings, generation, eligible):
    rows, width = embeddings.shape
    mult = smoothing_divisor / math.sqrt(width)
    keys = lax.all_gather(embeddings, "loop", axis=0, tiled=True)
    key_gen = lax.all_gather(generation, "loop", axis=0, tiled=True)
    key_flag = lax.all_gather(eligible, "loop", axis=0, tiled=True)
    scores = jnp.dot(embeddings, keys.T, preferred_element_type=jnp.float32) * mult
    valid = (key_gen[None, :] < generation[:, None]) & (key_flag[None, :] == 1)
    masked = jnp.where(valid, scores, -jnp.inf)
    peak = jnp.maximum(jnp.max(masked, axis=1), 0.0)
    expo = jnp.where(valid, jnp.exp(scores - peak[:, None]), jnp.float32(0.0))
    total = jnp.exp(-peak) + jnp.sum(expo, axis=1)
    summed = jnp.dot(expo.astype(jnp.bfloat16), keys, preferred_element_type=jnp.float32)
    return (summed / total[:, None]).astype(jnp.bfloat16), peak


def solution(mesh):
    n = mesh.shape["loop"]
    body = functools.partial(ring_body, n) if n <= 16 else gathered_body
    placed = (P(("groups", "loop"), None), P(("groups", "loop")), P(("groups", "loop")))
    return jax.shard_map(
        body,
        mesh=mesh,
        in_specs=placed,
        out_specs=(P(("groups", "loop"), None), P(("groups", "loop"))),
        check_vma=False,
    )
```

```python
import functools
import math

import jax
import jax.numpy as jnp
from jax import lax
from jax.experimental import pallas as pl
from jax.experimental.pallas import tpu as pltpu
from jax.sharding import PartitionSpec as P


smoothing_divisor = 3.0
CODE_LIMIT = 4 << 20


def ring_of_chips(chips):
    across = max(k for k in range(1, int(math.isqrt(chips)) + 1) if chips % k == 0)
    down = chips // across
    order = [(0, 0)]
    for r in range(down):
        columns = range(1, across)
        order += [(r, q) for q in (columns if r % 2 == 0 else reversed(columns))]
    order += [(r, 0) for r in range(down - 1, 0, -1)]
    return [r * across + q for r, q in order]


def swaps(ring):
    size = len(ring)
    even, odd = {}, {}
    for k in range(size):
        even[ring[k]] = ring[k ^ 1]
        odd[ring[k]] = ring[(((k - 1) ^ 1) + 1) % size]
    return even, odd


def code_kernel(x_hbm, flag_hbm, gen_hbm, x_ref, early_ref, late_ref, gen_ref, flag_ref, sems):
    rows = x_ref.shape[0]
    half = rows // 2
    flag_copy = pltpu.make_async_copy(flag_hbm, flag_ref, sems.at[0])
    flag_copy.start()
    x_copy = pltpu.make_async_copy(x_hbm, x_ref, sems.at[1])
    x_copy.start()
    gen_copy = pltpu.make_async_copy(gen_hbm, gen_ref, sems.at[2])
    gen_copy.start()
    flag_copy.wait()
    row_id = lax.broadcasted_iota(jnp.int32, (rows, rows), 0)
    col_id = lax.broadcasted_iota(jnp.int32, (rows, rows), 1)
    flags = jnp.broadcast_to(flag_ref[...], (rows, rows))
    flag = jnp.sum(jnp.where(row_id == col_id, flags, 0), axis=1, keepdims=True)
    bad = (flag != 1) & (lax.broadcasted_iota(jnp.int32, (rows, 128), 1) == 0)
    x_copy.wait()
    head = jnp.where(bad, jnp.float32(jnp.nan), x_ref[:, :128].astype(jnp.float32)).astype(jnp.bfloat16)
    for k, out_ref in enumerate((early_ref, late_ref)):
        out_ref[:, :128] = head[k * half : (k + 1) * half]
        out_ref[:, 128:] = x_ref[k * half : (k + 1) * half, 128:]
    gen_copy.wait()


def later_bits(me, bits):
    word = jnp.int32(0)
    for i, b in enumerate(bits):
        word = jnp.where(me == i, jnp.int32(b), word)
    return word


def scores_into(score_ref, at, mult, x, keys_ref, word, ids, gen_ref):
    rows = x.shape[0]
    half = rows // 2
    dims = (((1,), (1,)), ((), ()))
    row_id = lax.broadcasted_iota(jnp.int32, (rows, rows), 0)
    col_id = lax.broadcasted_iota(jnp.int32, (rows, rows), 1)
    late_q, late_k = row_id >= half, col_id >= half
    keys = jnp.concatenate([r[...] for r in keys_ref], axis=0)
    s = lax.dot_general(x, keys, dims, preferred_element_type=jnp.float32) * mult
    top = None
    for k, chunk in enumerate(ids):
        t = s[:, k * rows : (k + 1) * rows]
        if chunk == 0:
            gen_k = jnp.broadcast_to(gen_ref[...], (rows, rows))
            gen_q = jnp.sum(jnp.where(row_id == col_id, gen_k, 0), axis=1, keepdims=True)
            valid = gen_k < gen_q
        else:
            later = jnp.full((rows, rows), (word >> chunk) & 1) == 1
            valid = ((~late_k) & (late_q | ~later)) | (late_q & late_k & later)
        t = jnp.where(valid & (t == t), t, -jnp.inf)
        score_ref[:, at + k * rows : at + (k + 1) * rows] = t
        top = t if top is None else jnp.maximum(top, t)
    return top


def score_kernel(mult, bits, ids, me_ref, x_ref, gen_ref, *refs):
    keys, (score_ref, top_ref) = refs[:-2], refs[-2:]
    rows = x_ref.shape[0]
    x = x_ref[...]
    word = later_bits(me_ref[0], bits)
    top = None
    for k in range(0, len(ids), 2):
        t = scores_into(score_ref, k * rows, mult, x, keys[2 * k : 2 * k + 4], word, ids[k : k + 2], gen_ref)
        top = t if top is None else jnp.maximum(top, t)
    top_ref[...] = top


def finish_kernel(mult, bits, sizes, last_ids, me_ref, x_ref, gen_ref, *refs):
    count = len(sizes)
    scores, tops, refs = refs[:count], refs[count : 2 * count], refs[2 * count :]
    keys, (out_ref, peak_ref, last_ref) = refs[:-3], refs[-3:]
    rows, _ = x_ref.shape
    x = x_ref[...]
    last_keys = keys[-2 * len(last_ids) :]
    top = scores_into(last_ref, 0, mult, x, last_keys, later_bits(me_ref[0], bits), last_ids, gen_ref)
    for t in tops:
        top = jnp.maximum(top, t[...])
    peak = jnp.maximum(jnp.max(top, axis=1, keepdims=True), 0.0)
    pieces = [(ref, j * rows) for ref, size in zip((*scores, last_ref), (*sizes, len(last_ids))) for j in range(size)]
    total = jnp.exp(-peak)
    acc = [None, None]
    edge = 2 * rows
    for k in range(0, len(pieces), 2):
        s = jnp.concatenate([ref[:, at : at + rows] for ref, at in pieces[k : k + 2]], axis=1)
        expo = jnp.exp(s - peak)
        total = total + jnp.sum(expo, axis=1, keepdims=True)
        w = expo.astype(jnp.bfloat16)
        quad = keys[2 * k : 2 * k + 4]
        head = jnp.concatenate([v[:, :edge] for v in quad], axis=0)
        head = jnp.where(head == head, head, jnp.zeros_like(head))
        tail = jnp.concatenate([v[:, edge:] for v in quad], axis=0)
        for i, v in enumerate((head, tail)):
            t = jnp.dot(w, v, preferred_element_type=jnp.float32)
            acc[i] = t if acc[i] is None else acc[i] + t
    out_ref[:, :edge] = (acc[0] / total).astype(out_ref.dtype)
    out_ref[:, edge:] = (acc[1] / total).astype(out_ref.dtype)
    row_id = lax.broadcasted_iota(jnp.int32, (rows, rows), 0)
    col_id = lax.broadcasted_iota(jnp.int32, (rows, rows), 1)
    peak_ref[...] = jnp.sum(jnp.where(row_id == col_id, peak, 0.0), axis=0, keepdims=True)


def ring_body(n, embeddings, generation, eligible):
    rows, width = embeddings.shape
    half = rows // 2
    mult = smoothing_divisor / math.sqrt(width)
    maps = swaps(ring_of_chips(n // 2))
    me = lax.axis_index("loop").reshape(1)
    vmem = pl.BlockSpec(memory_space=pltpu.VMEM)
    smem = pl.BlockSpec(memory_space=pltpu.SMEM)
    hbm = pl.BlockSpec(memory_space=pltpu.MemorySpace.HBM)
    bf16 = lambda r: jax.ShapeDtypeStruct((r, width), jnp.bfloat16)

    def swap(kind, v):
        return lax.ppermute(v, "loop", [(i, maps[kind][i // 2] * 2 + i % 2) for i in range(n)])

    def other_core(v):
        return lax.ppermute(v, "loop", [(i, i ^ 1) for i in range(n)])

    x, early, late, gen = pl.pallas_call(
        code_kernel,
        out_shape=(bf16(rows), bf16(half), bf16(half), jax.ShapeDtypeStruct((1, rows), jnp.int32)),
        in_specs=[hbm] * 3,
        out_specs=(vmem,) * 4,
        scratch_shapes=[pltpu.VMEM((1, rows), jnp.int32), pltpu.SemaphoreType.DMA((3,))],
        compiler_params=pltpu.CompilerParams(vmem_limit_bytes=CODE_LIMIT),
        name="code",
    )(embeddings, eligible.reshape(1, rows), generation.reshape(1, rows))

    steps = n // 4
    parts, paths = [[early, late]], [[]]
    held = [parts[0], parts[0]]
    for step in range(steps):
        sent = [held[1], held[0]] if step else held
        paths += [[(kind + k) % 2 for k in range(step + 1)] for kind in (0, 1)][: 1 if step == steps - 1 else 2]
        held = [[None, None], [None, None]]
        for part in (0, 1):
            for kind in (0, 1) if step < steps - 1 else (part,):
                held[kind][part] = swap(kind, sent[kind][part])
        parts += held if step < steps - 1 else [[held[0][0], held[1][1]]]
    across = []
    for k, chunk in enumerate(parts):
        across.append([])
        for part in (0, 1):
            across[k].append(other_core(chunk[part]))
    bits = []
    for i in range(n):
        word = 0
        for k, path in enumerate(paths):
            chip = i // 2
            for kind in path:
                chip = maps[kind][chip]
            for j, source in ((k, chip * 2 + i % 2), (n // 2 + k, chip * 2 + 1 - i % 2)):
                word |= int(source > i) << j
        bits.append(word)
    bits = tuple(bits)
    keys_of = dict(enumerate(parts + across))

    limit = pltpu.CompilerParams(vmem_limit_bytes=8 << 20)

    def score(ids):
        columns = rows * len(ids)
        return pl.pallas_call(
            functools.partial(score_kernel, mult, bits, ids),
            out_shape=(
                jax.ShapeDtypeStruct((rows, columns), jnp.float32),
                jax.ShapeDtypeStruct((rows, rows), jnp.float32),
            ),
            in_specs=[smem] + [vmem] * (2 + 2 * len(ids)),
            out_specs=(vmem, vmem),
            compiler_params=limit,
            cost_estimate=pl.CostEstimate(flops=2 * rows * columns * width, bytes_accessed=0, transcendentals=0),
        )(me, x, gen, *[v for i in ids for v in keys_of[i]])

    chunks = n // 2
    last = chunks - 1
    early_ids = (0, 1, 2, *range(chunks, chunks + 3))
    late_ids = (last - 2, last - 1)
    middle_ids = tuple(i for i in range(3, last - 2)) + tuple(i for i in range(chunks + 3, chunks + last - 2)) + late_ids
    late_ids = tuple(chunks + i for i in late_ids) + (last,)
    plan = (early_ids, middle_ids, late_ids)
    scored = []
    for ids in plan:
        scored.append(score(ids))
    last_ids = (chunks + last,)
    out, peak = pl.pallas_call(
        functools.partial(finish_kernel, mult, bits, tuple(len(ids) for ids in plan), last_ids),
        out_shape=(bf16(rows), jax.ShapeDtypeStruct((1, rows), jnp.float32)),
        in_specs=[smem] + [vmem] * (8 + 4 * chunks),
        out_specs=(vmem, vmem),
        scratch_shapes=[pltpu.VMEM((rows, rows), jnp.float32)],
        compiler_params=limit,
        name="finish",
    )(me, x, gen, *[s for s, _ in scored], *[t for _, t in scored], *[v for ids in (*plan, last_ids) for i in ids for v in keys_of[i]])
    return out, peak.reshape(rows)


def gathered_body(embeddings, generation, eligible):
    _, width = embeddings.shape
    mult = smoothing_divisor / math.sqrt(width)
    keys = lax.all_gather(embeddings, "loop", axis=0, tiled=True)
    key_gen = lax.all_gather(generation, "loop", axis=0, tiled=True)
    key_flag = lax.all_gather(eligible, "loop", axis=0, tiled=True)
    scores = jnp.dot(embeddings, keys.T, preferred_element_type=jnp.float32) * mult
    valid = (key_gen[None, :] < generation[:, None]) & (key_flag[None, :] == 1)
    masked = jnp.where(valid, scores, -jnp.inf)
    peak = jnp.maximum(jnp.max(masked, axis=1), 0.0)
    expo = jnp.where(valid, jnp.exp(scores - peak[:, None]), jnp.float32(0.0))
    total = jnp.exp(-peak) + jnp.sum(expo, axis=1)
    summed = jnp.dot(expo.astype(jnp.bfloat16), keys, preferred_element_type=jnp.float32)
    return (summed / total[:, None]).astype(jnp.bfloat16), peak


def solution(mesh):
    n = mesh.shape["loop"]
    placed = (P(("groups", "loop"), None), P(("groups", "loop")), P(("groups", "loop")))
    small = n <= 16

    def body(*args):
        return ring_body(n, *args) if small else gathered_body(*args)

    return jax.shard_map(
        body,
        mesh=mesh,
        in_specs=placed,
        out_specs=(P(("groups", "loop"), None), P(("groups", "loop"))),
        check_vma=False,
    )
```

```python
import functools
import math

import jax
import jax.numpy as jnp
from jax import lax
from jax.experimental import pallas as pl
from jax.experimental.pallas import tpu as pltpu
from jax.sharding import PartitionSpec as P


smoothing_divisor = 3.0
CODE_LIMIT = 4 << 20


def ring_of_chips(chips):
    across = max(k for k in range(1, int(math.isqrt(chips)) + 1) if chips % k == 0)
    down = chips // across
    order = [(0, 0)]
    for r in range(down):
        columns = range(1, across)
        order += [(r, q) for q in (columns if r % 2 == 0 else reversed(columns))]
    order += [(r, 0) for r in range(down - 1, 0, -1)]
    return [r * across + q for r, q in order]


def swaps(ring):
    size = len(ring)
    even, odd = {}, {}
    for k in range(size):
        even[ring[k]] = ring[k ^ 1]
        odd[ring[k]] = ring[(((k - 1) ^ 1) + 1) % size]
    return even, odd


def code_kernel(x_hbm, flag_hbm, gen_hbm, x_ref, early_ref, late_ref, gen_ref, flag_ref, sems):
    rows = x_ref.shape[0]
    half = rows // 2
    flag_copy = pltpu.make_async_copy(flag_hbm, flag_ref, sems.at[0])
    flag_copy.start()
    x_copy = pltpu.make_async_copy(x_hbm, x_ref, sems.at[1])
    x_copy.start()
    gen_copy = pltpu.make_async_copy(gen_hbm, gen_ref, sems.at[2])
    gen_copy.start()
    flag_copy.wait()
    row_id = lax.broadcasted_iota(jnp.int32, (rows, rows), 0)
    col_id = lax.broadcasted_iota(jnp.int32, (rows, rows), 1)
    flags = jnp.broadcast_to(flag_ref[...], (rows, rows))
    flag = jnp.sum(jnp.where(row_id == col_id, flags, 0), axis=1, keepdims=True)
    bad = (flag != 1) & (lax.broadcasted_iota(jnp.int32, (rows, 128), 1) == 0)
    x_copy.wait()
    head = jnp.where(bad, jnp.float32(jnp.nan), x_ref[:, :128].astype(jnp.float32)).astype(jnp.bfloat16)
    for k, out_ref in enumerate((early_ref, late_ref)):
        out_ref[:, :128] = head[k * half : (k + 1) * half]
        out_ref[:, 128:] = x_ref[k * half : (k + 1) * half, 128:]
    gen_copy.wait()


def later_bits(me, bits):
    word = jnp.int32(0)
    for i, b in enumerate(bits):
        word = jnp.where(me == i, jnp.int32(b), word)
    return word


def scores_into(score_ref, at, mult, x, keys_ref, word, ids, gen_ref):
    rows = x.shape[0]
    half = rows // 2
    dims = (((1,), (1,)), ((), ()))
    row_id = lax.broadcasted_iota(jnp.int32, (rows, rows), 0)
    col_id = lax.broadcasted_iota(jnp.int32, (rows, rows), 1)
    late_q, late_k = row_id >= half, col_id >= half
    keys = jnp.concatenate([r[...] for r in keys_ref], axis=0)
    s = lax.dot_general(x, keys, dims, preferred_element_type=jnp.float32) * mult
    top = None
    for k, chunk in enumerate(ids):
        t = s[:, k * rows : (k + 1) * rows]
        if chunk == 0:
            gen_k = jnp.broadcast_to(gen_ref[...], (rows, rows))
            gen_q = jnp.sum(jnp.where(row_id == col_id, gen_k, 0), axis=1, keepdims=True)
            valid = gen_k < gen_q
        else:
            later = jnp.full((rows, rows), (word >> chunk) & 1) == 1
            valid = ((~late_k) & (late_q | ~later)) | (late_q & late_k & later)
        t = jnp.where(valid & (t == t), t, -jnp.inf)
        score_ref[:, at + k * rows : at + (k + 1) * rows] = t
        top = t if top is None else jnp.maximum(top, t)
    return top


def score_kernel(mult, bits, ids, me_ref, x_ref, gen_ref, *refs):
    keys, (score_ref, top_ref) = refs[:-2], refs[-2:]
    rows = x_ref.shape[0]
    x = x_ref[...]
    word = later_bits(me_ref[0], bits)
    top = None
    for k in range(0, len(ids), 2):
        t = scores_into(score_ref, k * rows, mult, x, keys[2 * k : 2 * k + 4], word, ids[k : k + 2], gen_ref)
        top = t if top is None else jnp.maximum(top, t)
    top_ref[...] = top


def finish_kernel(mult, bits, sizes, last_ids, me_ref, x_ref, gen_ref, *refs):
    count = len(sizes)
    scores, tops, refs = refs[:count], refs[count : 2 * count], refs[2 * count :]
    keys, (out_ref, peak_ref, last_ref) = refs[:-3], refs[-3:]
    rows, _ = x_ref.shape
    x = x_ref[...]
    last_keys = keys[-2 * len(last_ids) :]
    top = scores_into(last_ref, 0, mult, x, last_keys, later_bits(me_ref[0], bits), last_ids, gen_ref)
    for t in tops:
        top = jnp.maximum(top, t[...])
    peak = jnp.maximum(jnp.max(top, axis=1, keepdims=True), 0.0)
    pieces = [(ref, j * rows) for ref, size in zip((*scores, last_ref), (*sizes, len(last_ids))) for j in range(size)]
    total = jnp.exp(-peak)
    acc = [None, None]
    edge = 2 * rows
    for k in range(0, len(pieces), 16):
        s = jnp.concatenate([ref[:, at : at + rows] for ref, at in pieces[k : k + 16]], axis=1)
        expo = jnp.exp(s - peak)
        total = total + jnp.sum(expo, axis=1, keepdims=True)
        w = expo.astype(jnp.bfloat16)
        quad = keys[2 * k : 2 * k + 32]
        head = jnp.concatenate([v[:, :edge] for v in quad], axis=0)
        head = jnp.where(head == head, head, jnp.zeros_like(head))
        tail = jnp.concatenate([v[:, edge:] for v in quad], axis=0)
        for i, v in enumerate((head, tail)):
            t = jnp.dot(w, v, preferred_element_type=jnp.float32)
            acc[i] = t if acc[i] is None else acc[i] + t
    out_ref[:, :edge] = (acc[0] / total).astype(out_ref.dtype)
    out_ref[:, edge:] = (acc[1] / total).astype(out_ref.dtype)
    row_id = lax.broadcasted_iota(jnp.int32, (rows, rows), 0)
    col_id = lax.broadcasted_iota(jnp.int32, (rows, rows), 1)
    peak_ref[...] = jnp.sum(jnp.where(row_id == col_id, peak, 0.0), axis=0, keepdims=True)


def ring_body(n, embeddings, generation, eligible):
    rows, width = embeddings.shape
    half = rows // 2
    mult = smoothing_divisor / math.sqrt(width)
    maps = swaps(ring_of_chips(n // 2))
    me = lax.axis_index("loop").reshape(1)
    vmem = pl.BlockSpec(memory_space=pltpu.VMEM)
    smem = pl.BlockSpec(memory_space=pltpu.SMEM)
    hbm = pl.BlockSpec(memory_space=pltpu.MemorySpace.HBM)
    bf16 = lambda r: jax.ShapeDtypeStruct((r, width), jnp.bfloat16)

    def swap(kind, v):
        return lax.ppermute(v, "loop", [(i, maps[kind][i // 2] * 2 + i % 2) for i in range(n)])

    def other_core(v):
        return lax.ppermute(v, "loop", [(i, i ^ 1) for i in range(n)])

    x, early, late, gen = pl.pallas_call(
        code_kernel,
        out_shape=(bf16(rows), bf16(half), bf16(half), jax.ShapeDtypeStruct((1, rows), jnp.int32)),
        in_specs=[hbm] * 3,
        out_specs=(vmem,) * 4,
        scratch_shapes=[pltpu.VMEM((1, rows), jnp.int32), pltpu.SemaphoreType.DMA((3,))],
        compiler_params=pltpu.CompilerParams(vmem_limit_bytes=CODE_LIMIT),
        name="code",
    )(embeddings, eligible.reshape(1, rows), generation.reshape(1, rows))

    steps = n // 4
    parts, paths = [[early, late]], [[]]
    held = [parts[0], parts[0]]
    for step in range(steps):
        sent = [held[1], held[0]] if step else held
        paths += [[(kind + k) % 2 for k in range(step + 1)] for kind in (0, 1)][: 1 if step == steps - 1 else 2]
        held = [[None, None], [None, None]]
        for part in (0, 1):
            for kind in (0, 1) if step < steps - 1 else (part,):
                held[kind][part] = swap(kind, sent[kind][part])
        parts += held if step < steps - 1 else [[held[0][0], held[1][1]]]
    across = []
    for k, chunk in enumerate(parts):
        across.append([])
        for part in (0, 1):
            across[k].append(other_core(chunk[part]))
    bits = []
    for i in range(n):
        word = 0
        for k, path in enumerate(paths):
            chip = i // 2
            for kind in path:
                chip = maps[kind][chip]
            for j, source in ((k, chip * 2 + i % 2), (n // 2 + k, chip * 2 + 1 - i % 2)):
                word |= int(source > i) << j
        bits.append(word)
    bits = tuple(bits)
    keys_of = dict(enumerate(parts + across))

    limit = pltpu.CompilerParams(vmem_limit_bytes=8 << 20)

    def score(ids):
        columns = rows * len(ids)
        return pl.pallas_call(
            functools.partial(score_kernel, mult, bits, ids),
            out_shape=(
                jax.ShapeDtypeStruct((rows, columns), jnp.float32),
                jax.ShapeDtypeStruct((rows, rows), jnp.float32),
            ),
            in_specs=[smem] + [vmem] * (2 + 2 * len(ids)),
            out_specs=(vmem, vmem),
            compiler_params=limit,
            cost_estimate=pl.CostEstimate(flops=2 * rows * columns * width, bytes_accessed=0, transcendentals=0),
        )(me, x, gen, *[v for i in ids for v in keys_of[i]])

    chunks = n // 2
    last = chunks - 1
    early_ids = (0, 1, 2, *range(chunks, chunks + 3))
    late_ids = (last - 2, last - 1)
    middle_ids = tuple(i for i in range(3, last - 2)) + tuple(i for i in range(chunks + 3, chunks + last - 2)) + late_ids
    late_ids = tuple(chunks + i for i in late_ids) + (last,)
    plan = (early_ids, middle_ids, late_ids)
    scored = []
    for ids in plan:
        scored.append(score(ids))
    last_ids = (chunks + last,)
    out, peak = pl.pallas_call(
        functools.partial(finish_kernel, mult, bits, tuple(len(ids) for ids in plan), last_ids),
        out_shape=(bf16(rows), jax.ShapeDtypeStruct((1, rows), jnp.float32)),
        in_specs=[smem] + [vmem] * (8 + 4 * chunks),
        out_specs=(vmem, vmem),
        scratch_shapes=[pltpu.VMEM((rows, rows), jnp.float32)],
        compiler_params=limit,
        name="finish",
    )(me, x, gen, *[s for s, _ in scored], *[t for _, t in scored], *[v for ids in (*plan, last_ids) for i in ids for v in keys_of[i]])
    return out, peak.reshape(rows)


def gathered_body(embeddings, generation, eligible):
    _, width = embeddings.shape
    mult = smoothing_divisor / math.sqrt(width)
    keys = lax.all_gather(embeddings, "loop", axis=0, tiled=True)
    key_gen = lax.all_gather(generation, "loop", axis=0, tiled=True)
    key_flag = lax.all_gather(eligible, "loop", axis=0, tiled=True)
    scores = jnp.dot(embeddings, keys.T, preferred_element_type=jnp.float32) * mult
    valid = (key_gen[None, :] < generation[:, None]) & (key_flag[None, :] == 1)
    masked = jnp.where(valid, scores, -jnp.inf)
    peak = jnp.maximum(jnp.max(masked, axis=1), 0.0)
    expo = jnp.where(valid, jnp.exp(scores - peak[:, None]), jnp.float32(0.0))
    total = jnp.exp(-peak) + jnp.sum(expo, axis=1)
    summed = jnp.dot(expo.astype(jnp.bfloat16), keys, preferred_element_type=jnp.float32)
    return (summed / total[:, None]).astype(jnp.bfloat16), peak


def solution(mesh):
    n = mesh.shape["loop"]
    placed = (P(("groups", "loop"), None), P(("groups", "loop")), P(("groups", "loop")))
    small = n <= 16

    def body(*args):
        return ring_body(n, *args) if small else gathered_body(*args)

    return jax.shard_map(
        body,
        mesh=mesh,
        in_specs=placed,
        out_specs=(P(("groups", "loop"), None), P(("groups", "loop"))),
        check_vma=False,
    )
```
